128 devices in a mesh: req: 32 (over y, x, core), head: 4 (over z).
Axes of the slice: x: 4, y: 4, z: 4, core: 2. Of those that a mesh axis runs over, the one named last changes fastest.
Arguments:
- hidden_in: bfloat16 [1024, 5120], P('req'), may hold values from -60 to 60
- query: bfloat16 [1024, 4096], P('req', 'head'), may hold values from -12 to 12
- incoming_key: bfloat16 [1024, 1024], P('req', 'head'), may hold values from -6 to 6
- incoming_value: bfloat16 [1024, 1024], P('req', 'head'), may hold values from -6 to 6
- private_tail_keys: bfloat16 [1024, 160, 1024], P('req', None, 'head'), may hold values from -6 to 6
- private_tail_values: bfloat16 [1024, 160, 1024], P('req', None, 'head'), may hold values from -6 to 6
- group_prompt_keys: bfloat16 [96, 512, 1024], P('req', None, 'head'), may hold values from -6 to 6
- group_prompt_values: bfloat16 [96, 512, 1024], P('req', None, 'head'), may hold values from -6 to 6
- group_id: int32 [1024], P('req'), may hold values from 0 to 95, as said below
- prompt_len: int32 [96], P('req'), may hold values from 128 to 512, as said below
- tail_len: int32 [1024], P('req'), may hold values from 0 to 159, as said below
- out_proj: bfloat16 [4096, 5120], P('head'), may hold values from -0.5 to 0.5
- norm_gain: float32 [5120], replicated, may hold values from 0.1 to 1.9
- gate_proj: bfloat16 [5120, 32768], P(None, ('req', 'head')), may hold values from -0.078125 to 0.078125
- up_proj: bfloat16 [5120, 32768], P(None, ('req', 'head')), may hold values from -0.078125 to 0.078125
- down_proj: bfloat16 [32768, 5120], P('req', 'head'), may hold values from -0.03125 to 0.03125
Outputs:
- layer_out: bfloat16 [1024, 5120], P(('req', 'head'))
The draws below stay inside these ranges and needn't reach their ends.
Inputs may be any that keep to these rules, and one draw needn't show every extreme that they name: `group_id`: the prompt cache of group g is held by index g // 3 of req. Among the 32 requests of one index of req, at most 2 belong to groups held by any one index of req; in every draw one index of req holds the groups of exactly 2 requests of every index of req. `prompt_len`: some group's prompt fills all 512 positions. Request r's earlier private tokens are in slots 0 to tail_len[r] - 1; some request has 159 of them.
All inputs are finite; a program needn't handle non-finite values.
Results may differ from the reference program's by a relative error of at most 0.007.
Values may be sent and summed in bfloat16 or wider, within the bound.
No kernel may reach another device: no remote copies, remote signals or barrier semaphores. Data moves between devices by JAX's collectives and lax.ppermute only.
A program may use at most 128 MiB of HBM per device.

```python
import math
import jax
import jax.numpy as jnp
from jax import lax

D = 5120
QUERY_HEADS = 32
KEY_VALUE_HEADS = 8
HEAD_WIDTH = 128
FF = 32768
REQ_DEV = 32
PROMPT_LENGTH = 512
TAIL_SLOTS = 160
REQUEST_COUNT = 1024
GROUP_DEV = 3
PROMPT_GROUPS = 96
CAP = 2


def draw_query(key, part):
    value_rows = jnp.clip(jax.random.normal(jax.random.fold_in(key, 1), (REQUEST_COUNT, QUERY_HEADS * HEAD_WIDTH), jnp.float32), -6.0, 6.0)
    return value_rows.astype(jnp.bfloat16)


def draw_group_prompt_keys(key, part):
    value_rows = jnp.clip(jax.random.normal(jax.random.fold_in(key, 4), (PROMPT_GROUPS, PROMPT_LENGTH, KEY_VALUE_HEADS * HEAD_WIDTH), jnp.float32), -6.0, 6.0)
    return value_rows.astype(jnp.bfloat16)


def draw_hidden_in(key, part):
    base = jnp.clip(jax.random.normal(jax.random.fold_in(key, 6), (REQUEST_COUNT, D), jnp.float32), -6.0, 6.0)
    row_scale = 0.1 * jnp.exp(jax.random.uniform(jax.random.fold_in(key, 8), (REQUEST_COUNT, 1), jnp.float32) * math.log(10.0))
    col_scale = 0.3 * jnp.exp(jax.random.uniform(jax.random.fold_in(key, 9), (1, D), jnp.float32) * math.log(10.0))
    block_scale = jnp.repeat(jnp.exp(jax.random.uniform(jax.random.fold_in(key, 10), (8,), jnp.float32) * math.log(3.0)), D // 8)[None, :]
    return (base * row_scale * col_scale * block_scale).astype(jnp.bfloat16)


def draw_group_id(key, part):
    holders = REQUEST_COUNT // REQ_DEV
    tickets = holders * CAP
    hottest = jax.random.randint(jax.random.fold_in(key, 11), (), 0, holders)
    favour = jax.random.randint(jax.random.fold_in(key, 12), (holders,), 0, 4)
    ticket_ids = jnp.arange(tickets, dtype=jnp.int32)
    ticket_holder = ticket_ids // CAP

    def one_device(device):
        device_key = jax.random.fold_in(jax.random.fold_in(key, 13), device)
        noise = jax.random.randint(jax.random.fold_in(device_key, 1), (tickets,), 0, 32768)
        merit = noise + favour[ticket_holder] * 16384 + jnp.where(ticket_holder == hottest, 262144, 0)
        merit = merit * 1024 + ticket_ids
        chosen = lax.top_k(merit, REQ_DEV)[1]
        picked = ticket_holder[chosen]
        shuffled = jax.random.permutation(jax.random.fold_in(device_key, 2), picked)
        inner = jax.random.randint(jax.random.fold_in(device_key, 3), (REQ_DEV,), 0, GROUP_DEV)
        return shuffled * GROUP_DEV + inner
    every = jax.vmap(one_device)(jnp.arange(holders, dtype=jnp.int32))
    return every.reshape(REQUEST_COUNT).astype(jnp.int32)


def draw_prompt_len(key, part):
    lengths = jax.random.randint(jax.random.fold_in(key, 14), (PROMPT_GROUPS,), PROMPT_LENGTH // 4, PROMPT_LENGTH + 1)
    longest = jax.random.randint(jax.random.fold_in(key, 15), (), 0, PROMPT_GROUPS)
    return jnp.where(jnp.arange(PROMPT_GROUPS) == longest, PROMPT_LENGTH, lengths).astype(jnp.int32)


def draw_tail_len(key, part):
    devices = REQUEST_COUNT // REQ_DEV
    limit = jax.random.randint(jax.random.fold_in(key, 16), (devices, 1), TAIL_SLOTS // 4, TAIL_SLOTS + 1)
    lengths = jax.random.randint(jax.random.fold_in(key, 17), (devices, REQ_DEV), 0, limit)
    lengths = jnp.minimum(lengths, TAIL_SLOTS - 1).reshape(REQUEST_COUNT)
    longest = jax.random.randint(jax.random.fold_in(key, 18), (), 0, REQUEST_COUNT)
    return jnp.where(jnp.arange(REQUEST_COUNT) == longest, TAIL_SLOTS - 1, lengths).astype(jnp.int32)


def levels(key, extent, pieces, low, high):
    level, own = 1.0, jax.random.fold_in(key, 6)
    for dim, blocks in pieces:
        steps = jnp.exp(jax.random.uniform(jax.random.fold_in(own, dim), (blocks,), jnp.float32, low / len(pieces), high / len(pieces)))
        level = level * jnp.repeat(steps, extent[dim] // blocks).reshape([-1 if axis == dim else 1 for axis in range(len(extent))])
    return level


def gaussian(key, dims, spread, most, cuts=(), kind=jnp.bfloat16):
    loudness = levels(key, dims, cuts, -0.22, 0.18) if cuts else 1.0
    array = jax.random.normal(key, dims, jnp.float32) * spread * loudness
    return jnp.minimum(jnp.maximum(array, -most), most).astype(kind)


def setup_inputs(seed: int = 0) -> dict:
    key_list = jax.random.split(jax.random.key(seed), 17)
    hidden_in = draw_hidden_in(jax.random.fold_in(key_list[16], 71), 0)
    query = draw_query(jax.random.fold_in(key_list[16], 71), 0)
    incoming_key = gaussian(key_list[2], (REQUEST_COUNT, KEY_VALUE_HEADS * HEAD_WIDTH), 1.0, 6.0, ((0, 32), (1, 4)))
    incoming_value = gaussian(key_list[3], (REQUEST_COUNT, KEY_VALUE_HEADS * HEAD_WIDTH), 1.0, 6.0, ((0, 32), (1, 4)))
    private_tail_keys = gaussian(key_list[4], (REQUEST_COUNT, TAIL_SLOTS, KEY_VALUE_HEADS * HEAD_WIDTH), 1.0, 6.0, ((0, 32), (2, 4)))
    private_tail_values = gaussian(key_list[5], (REQUEST_COUNT, TAIL_SLOTS, KEY_VALUE_HEADS * HEAD_WIDTH), 1.0, 6.0, ((0, 32), (2, 4)))
    group_prompt_keys = draw_group_prompt_keys(jax.random.fold_in(key_list[16], 71), 0)
    group_prompt_values = gaussian(key_list[7], (PROMPT_GROUPS, PROMPT_LENGTH, KEY_VALUE_HEADS * HEAD_WIDTH), 1.0, 6.0, ((0, 32), (2, 4)))
    group_id = draw_group_id(jax.random.fold_in(key_list[16], 71), 0)
    prompt_len = draw_prompt_len(jax.random.fold_in(key_list[16], 71), 0)
    tail_len = draw_tail_len(jax.random.fold_in(key_list[16], 71), 0)
    out_proj = gaussian(key_list[11], (QUERY_HEADS * HEAD_WIDTH, D), HEAD_WIDTH ** -0.5, 0.5, ((0, 4),))
    norm_gain = jnp.clip(1.0 + 0.18 * jax.random.normal(key_list[12], (D,), jnp.float32), 0.1, 1.9)
    gate_proj = gaussian(key_list[13], (D, FF), D ** -0.5, 0.078125, ((1, 128),))
    up_proj = gaussian(key_list[14], (D, FF), D ** -0.5, 0.078125, ((1, 128),))
    down_proj = gaussian(key_list[15], (FF, D), FF ** -0.5, 0.03125, ((0, 32), (1, 4)))
    return {"hidden_in": hidden_in, "query": query, "incoming_key": incoming_key, "incoming_value": incoming_value, "private_tail_keys": private_tail_keys, "private_tail_values": private_tail_values, "group_prompt_keys": group_prompt_keys, "group_prompt_values": group_prompt_values, "group_id": group_id, "prompt_len": prompt_len, "tail_len": tail_len, "out_proj": out_proj, "norm_gain": norm_gain, "gate_proj": gate_proj, "up_proj": up_proj, "down_proj": down_proj}


MASKED_SCORE = -1e+30

def reference(hidden_in, query, incoming_key, incoming_value, private_tail_keys, private_tail_values, group_prompt_keys, group_prompt_values, group_id, prompt_len, tail_len, out_proj, norm_gain, gate_proj, up_proj, down_proj):
    each_key_value = QUERY_HEADS // KEY_VALUE_HEADS
    scale_of_scores = HEAD_WIDTH ** (-0.5)
    block_row_list = 32
    block_count = REQUEST_COUNT // block_row_list

    def attend(block_index):
        first_entry = (block_index * block_row_list).astype(jnp.int32)
        query_rows = lax.dynamic_slice_in_dim(query, first_entry, block_row_list, 0).astype(jnp.float32).reshape(block_row_list, KEY_VALUE_HEADS, each_key_value, HEAD_WIDTH)
        group_list = lax.dynamic_slice_in_dim(group_id, first_entry, block_row_list, 0)
        common_prompt_keys = group_prompt_keys[group_list].astype(jnp.float32).reshape(block_row_list, PROMPT_LENGTH, KEY_VALUE_HEADS, HEAD_WIDTH)
        common_prompt_values = group_prompt_values[group_list].astype(jnp.float32).reshape(block_row_list, PROMPT_LENGTH, KEY_VALUE_HEADS, HEAD_WIDTH)
        limits = prompt_len[group_list]
        shared_scores = jnp.einsum('bkrd,bpkd->bkrp', query_rows, common_prompt_keys) * scale_of_scores
        shared_live = (jnp.arange(PROMPT_LENGTH)[None, :] < limits[:, None])[:, None, None, :]
        masked = jnp.where(shared_live, shared_scores, MASKED_SCORE)
        shared_max = lax.optimization_barrier(jnp.max(masked, axis=-1))
        shared_exp = jnp.exp(masked - shared_max[..., None])
        shared_total = lax.optimization_barrier(jnp.sum(shared_exp, axis=-1))
        shared_weights = lax.optimization_barrier(shared_exp.astype(jnp.bfloat16)).astype(jnp.float32)
        shared_mix = jnp.einsum('bkrp,bpkd->bkrd', shared_weights, common_prompt_values)
        request_keys = lax.dynamic_slice_in_dim(private_tail_keys, first_entry, block_row_list, 0).astype(jnp.float32).reshape(block_row_list, TAIL_SLOTS, KEY_VALUE_HEADS, HEAD_WIDTH)
        request_values = lax.dynamic_slice_in_dim(private_tail_values, first_entry, block_row_list, 0).astype(jnp.float32).reshape(block_row_list, TAIL_SLOTS, KEY_VALUE_HEADS, HEAD_WIDTH)
        current_key = lax.dynamic_slice_in_dim(incoming_key, first_entry, block_row_list, 0).astype(jnp.float32).reshape(block_row_list, KEY_VALUE_HEADS, HEAD_WIDTH)
        current_value = lax.dynamic_slice_in_dim(incoming_value, first_entry, block_row_list, 0).astype(jnp.float32).reshape(block_row_list, KEY_VALUE_HEADS, HEAD_WIDTH)
        own_len = lax.dynamic_slice_in_dim(tail_len, first_entry, block_row_list, 0)
        tail_scores = jnp.einsum('bkrd,btkd->bkrt', query_rows, request_keys) * scale_of_scores
        current_scores = jnp.einsum('ivxg,ivg->ivx', query_rows, current_key) * scale_of_scores
        tail_live = (jnp.arange(TAIL_SLOTS)[None, :] < own_len[:, None])[:, None, None, :]
        tail_masked = jnp.where(tail_live, tail_scores, MASKED_SCORE)
        local_max = jnp.maximum(lax.optimization_barrier(jnp.max(tail_masked, axis=-1)), current_scores)
        tail_exp = jnp.exp(tail_masked - local_max[..., None])
        fresh_exp = jnp.exp(current_scores - local_max)
        local_total = lax.optimization_barrier(jnp.sum(tail_exp, axis=-1)) + fresh_exp
        tail_weights = lax.optimization_barrier(tail_exp.astype(jnp.bfloat16)).astype(jnp.float32)
        fresh_weights = lax.optimization_barrier(fresh_exp.astype(jnp.bfloat16)).astype(jnp.float32)
        local_mix = jnp.einsum('bkrt,btkd->bkrd', tail_weights, request_values) + fresh_weights[..., None] * current_value[:, :, None, :]
        highest = jnp.maximum(shared_max, local_max)
        shared_factor = jnp.exp(shared_max - highest)
        local_factor = jnp.exp(local_max - highest)
        numer = shared_mix * shared_factor[..., None] + local_mix * local_factor[..., None]
        denom = shared_total * shared_factor + local_total * local_factor
        return (numer / denom[..., None]).reshape(block_row_list, QUERY_HEADS * HEAD_WIDTH).astype(jnp.bfloat16)
    attention = lax.map(attend, jnp.arange(block_count)).reshape(REQUEST_COUNT, QUERY_HEADS * HEAD_WIDTH)
    projected = jnp.dot(attention, out_proj, preferred_element_type=jnp.float32)
    residual = (hidden_in.astype(jnp.float32) + projected).astype(jnp.bfloat16)
    resid_f = residual.astype(jnp.float32)
    normed = (resid_f * lax.rsqrt(lax.optimization_barrier(jnp.mean(resid_f * resid_f, axis=-1, keepdims=True)) + 1e-05) * norm_gain).astype(jnp.bfloat16)
    gate_vals = jnp.dot(normed, gate_proj, preferred_element_type=jnp.float32)
    up_vals = jnp.dot(normed, up_proj, preferred_element_type=jnp.float32)
    hidden = (jax.nn.silu(gate_vals) * up_vals).astype(jnp.bfloat16)
    lowered = jnp.dot(hidden, down_proj, preferred_element_type=jnp.float32)
    return (resid_f + lowered).astype(jnp.bfloat16)
```

```python
import jax
import jax.numpy as jnp
from jax import lax
from jax.sharding import PartitionSpec as P

QUERY_HEADS = 32
KEY_VALUE_HEADS = 8
HEAD_WIDTH = 128


MASKED_SCORE = -1e30


def shards(
    hidden_in,
    query,
    incoming_key,
    incoming_value,
    private_tail_keys,
    private_tail_values,
    group_prompt_keys,
    group_prompt_values,
    group_id,
    prompt_len,
    tail_len,
    out_proj,
    norm_gain,
    gate_proj,
    up_proj,
    down_proj,
):
    n_req = lax.axis_size("req")
    n_head = lax.axis_size("head")
    row_count = query.shape[0]
    kv_local = incoming_key.shape[1] // HEAD_WIDTH
    each_key_value = QUERY_HEADS // KEY_VALUE_HEADS
    group_count = prompt_len.shape[0]
    prompt_size = group_prompt_keys.shape[1]
    tail_size = private_tail_keys.shape[1]
    slot_cap = 2 * row_count // n_req
    slot_total = n_req * slot_cap
    scale_of_scores = HEAD_WIDTH ** (-0.5)
    col_width = query.shape[1]
    head_local = kv_local * each_key_value
    holder = group_id // group_count
    local_group = group_id - holder * group_count
    holder_hot = (holder[:, None] == jnp.arange(n_req)[None, :]).astype(jnp.int32)
    before = jnp.cumsum(holder_hot, axis=0) - holder_hot
    order_in = jnp.sum(before * holder_hot, axis=1)
    slot_of = holder * slot_cap + order_in
    placing = slot_of[:, None] == jnp.arange(slot_total)[None, :]
    sent_rows = jnp.einsum(
        "rs,rc->sc",
        placing.astype(jnp.bfloat16),
        jnp.concatenate(
            [
                query,
                jnp.broadcast_to(
                    (local_group[:, None] + 1).astype(jnp.bfloat16), (row_count, HEAD_WIDTH)
                ),
            ],
            axis=1,
        ),
        preferred_element_type=jnp.float32,
    ).astype(jnp.bfloat16)
    keys_all = group_prompt_keys.reshape(group_count * prompt_size, kv_local, HEAD_WIDTH)
    values_all = group_prompt_values.reshape(group_count * prompt_size, kv_local, HEAD_WIDTH)
    key_group = jnp.arange(group_count * prompt_size) // prompt_size
    key_live = jnp.arange(group_count * prompt_size) % prompt_size < jnp.repeat(
        prompt_len, prompt_size
    )
    recv = lax.all_to_all(
        sent_rows.reshape(n_req, slot_cap, col_width + HEAD_WIDTH),
        "req",
        split_axis=0,
        concat_axis=0,
        tiled=True,
    ).reshape(slot_total, col_width + HEAD_WIDTH)
    recv_group = recv[:, col_width].astype(jnp.int32) - 1
    flat_query = recv[:, :col_width].reshape(slot_total, kv_local, each_key_value, HEAD_WIDTH)
    scores = (
        jnp.einsum("nkrd,pkd->nkrp", flat_query, keys_all, preferred_element_type=jnp.float32)
        * scale_of_scores
    )
    usable = (recv_group[:, None] == key_group[None, :]) & key_live[
        None, :
    ]
    masked = jnp.where(usable[:, None, None, :], scores, MASKED_SCORE)
    largest = jnp.max(masked, axis=-1)
    weights = jnp.exp(masked - largest[..., None])
    totals = jnp.sum(weights, axis=-1)
    mixture = jnp.einsum(
        "nkrp,pkd->nkrd",
        weights.astype(jnp.bfloat16),
        values_all,
        preferred_element_type=jnp.float32,
    )
    back = lax.all_to_all(
        jnp.concatenate(
            [
                mixture.reshape(slot_total, col_width),
                largest.reshape(slot_total, head_local),
                totals.reshape(slot_total, head_local),
                jnp.zeros((slot_total, HEAD_WIDTH - 2 * head_local), jnp.float32),
            ],
            axis=1,
        ).reshape(n_req, slot_cap, col_width + HEAD_WIDTH),
        "req",
        split_axis=0,
        concat_axis=0,
        tiled=True,
    )
    shared = jnp.take(back.reshape(slot_total, col_width + HEAD_WIDTH), slot_of, axis=0)
    shared_mix = shared[:, :col_width].reshape(row_count, kv_local, each_key_value, HEAD_WIDTH)
    shared_max = shared[:, col_width : col_width + head_local].reshape(
        row_count, kv_local, each_key_value
    )
    shared_total = shared[:, col_width + head_local : col_width + 2 * head_local].reshape(
        row_count, kv_local, each_key_value
    )
    query_rows = query.reshape(row_count, kv_local, each_key_value, HEAD_WIDTH)
    request_keys = private_tail_keys.reshape(row_count, tail_size, kv_local, HEAD_WIDTH)
    request_values = private_tail_values.reshape(row_count, tail_size, kv_local, HEAD_WIDTH)
    tail_scores = (
        jnp.einsum("bkrd,btkd->bkrt", query_rows, request_keys, preferred_element_type=jnp.float32)
        * scale_of_scores
    )
    current_scores = (
        jnp.einsum(
            "ivxg,ivg->ivx",
            query_rows,
            incoming_key.reshape(row_count, kv_local, HEAD_WIDTH),
            preferred_element_type=jnp.float32,
        )
        * scale_of_scores
    )
    tail_live = (jnp.arange(tail_size)[None, :] < tail_len[:, None])[:, None, None, :]
    tail_masked = jnp.where(tail_live, tail_scores, MASKED_SCORE)
    local_max = jnp.maximum(jnp.max(tail_masked, axis=-1), current_scores)
    tail_exp = jnp.exp(tail_masked - local_max[..., None])
    fresh_exp = jnp.exp(current_scores - local_max)
    local_total = jnp.sum(tail_exp, axis=-1) + fresh_exp
    fresh_weights = lax.optimization_barrier(fresh_exp.astype(jnp.bfloat16)).astype(jnp.float32)
    fresh_vals = incoming_value.reshape(row_count, kv_local, HEAD_WIDTH).astype(jnp.float32)
    local_mix = (
        jnp.einsum(
            "bkrt,btkd->bkrd",
            tail_exp.astype(jnp.bfloat16),
            request_values,
            preferred_element_type=jnp.float32,
        )
        + fresh_weights[..., None] * fresh_vals[:, :, None, :]
    )
    highest = jnp.maximum(shared_max, local_max)
    shared_factor = jnp.exp(shared_max - highest)
    local_factor = jnp.exp(local_max - highest)
    numer = shared_mix * shared_factor[..., None] + local_mix * local_factor[..., None]
    denom = shared_total * shared_factor + local_total * local_factor
    attention = (numer / denom[..., None]).reshape(row_count, col_width).astype(jnp.bfloat16)
    projected = jnp.dot(attention, out_proj, preferred_element_type=jnp.float32)
    sub_rows = row_count // n_head
    head_index = lax.axis_index("head")
    parts = lax.all_to_all(
        projected.reshape(n_head, sub_rows, -1), "head", split_axis=0, concat_axis=0, tiled=True
    )
    own_in = lax.dynamic_slice_in_dim(hidden_in, head_index * sub_rows, sub_rows, 0)
    residual = (own_in.astype(jnp.float32) + jnp.sum(parts, axis=0)).astype(jnp.bfloat16)
    resid_f = residual.astype(jnp.float32)
    segment = lax.all_gather(
        (
            resid_f
            * lax.rsqrt(jnp.mean(resid_f * resid_f, axis=-1, keepdims=True) + 1e-05)
            * norm_gain
        ).astype(jnp.bfloat16),
        ("req", "head"),
        axis=0,
        tiled=True,
    )
    gate_vals = jnp.dot(segment, gate_proj, preferred_element_type=jnp.float32)
    up_vals = jnp.dot(segment, up_proj, preferred_element_type=jnp.float32)
    hidden = (jax.nn.silu(gate_vals) * up_vals).astype(jnp.bfloat16)
    hidden_all = lax.all_gather(hidden, "head", axis=0)
    down_parts = down_proj.reshape(n_head, hidden.shape[1], -1)
    lowered = lax.psum_scatter(
        jnp.einsum("hru,huc->rc", hidden_all, down_parts, preferred_element_type=jnp.float32),
        "req",
        scatter_dimension=0,
        tiled=True,
    )
    lowered = lax.all_to_all(lowered, "head", split_axis=0, concat_axis=1, tiled=True)
    return (resid_f + lowered).astype(jnp.bfloat16)


def solution(mesh):
    return jax.shard_map(
        shards,
        mesh=mesh,
        in_specs=(
            P("req", None),
            P("req", "head"),
            P("req", "head"),
            P("req", "head"),
            P("req", None, "head"),
            P("req", None, "head"),
            P("req", None, "head"),
            P("req", None, "head"),
            P("req"),
            P("req"),
            P("req"),
            P("head", None),
            P(),
            P(None, ("req", "head")),
            P(None, ("req", "head")),
            P("req", "head"),
        ),
        out_specs=P(("req", "head"), None),
        check_vma=False,
    )
```

```python
import functools

import jax
import jax.numpy as jnp
from jax import lax
from jax.experimental import pallas as pl
from jax.experimental.pallas import tpu as pltpu
from jax.sharding import Mesh, PartitionSpec as P

QUERY_HEADS = 32
KEY_VALUE_HEADS = 8
HEAD_WIDTH = 128


MASKED_SCORE = -1e30


REQ = ("y", "x", "core")
RING = 4
PIECE = 64
K_BLOCK = 512


def shift(value, axis, step):
    size = lax.axis_size(axis)
    return lax.ppermute(value, axis, [(i, (i + step) % size) for i in range(size)])


def ring_pieces(value, axis):
    return [value] + [shift(value, axis, step) for step in (1, 2, 3)]


def mlp_in_kernel(*refs, n):
    rows, (gate_a, gate_b, up_a, up_b, out, acc) = refs[:n], refs[n:]
    step = pl.program_id(0)
    block = jnp.concatenate([r[...] for r in rows], axis=0)
    width = gate_a.shape[1]
    for i, w in enumerate((gate_a, gate_b, up_a, up_b)):
        part = jnp.dot(block, w[...], preferred_element_type=jnp.float32)
        cols = pl.ds(i * width, width)

        @pl.when(step == 0)
        def _():
            acc[:, cols] = part

        @pl.when(step > 0)
        def _():
            acc[:, cols] += part

    @pl.when(step == pl.num_programs(0) - 1)
    def _():
        gate = acc[:, : 2 * width]
        out[...] = (gate / (1.0 + jnp.exp(-gate)) * acc[:, 2 * width :]).astype(out.dtype)


def mlp_in(pieces, weights):
    n = len(pieces)
    depth, width = weights[0].shape
    rows = sum(p.shape[0] for p in pieces)
    return pl.pallas_call(
        functools.partial(mlp_in_kernel, n=n),
        grid=(depth // K_BLOCK,),
        in_specs=[pl.BlockSpec((p.shape[0], K_BLOCK), lambda k: (0, k)) for p in pieces]
        + [pl.BlockSpec((K_BLOCK, width), lambda k: (k, 0))] * 4,
        out_specs=pl.BlockSpec((rows, 2 * width), lambda k: (0, 0)),
        out_shape=jax.ShapeDtypeStruct((rows, 2 * width), jnp.bfloat16),
        scratch_shapes=[pltpu.VMEM((rows, 4 * width), jnp.float32)],
        name="mlp_in",
    )(*pieces, *weights)


def mlp_out_kernel(index, *refs, groups):
    hidden, (down_a, down_b, out, acc) = refs[: RING * len(groups)], refs[RING * len(groups) :]
    step = pl.program_id(0)
    half = down_a.shape[0]
    for i in range(RING):

        @pl.when(step == i)
        def _():
            block = jnp.concatenate([hidden[g * RING + i][...] for g in range(len(groups))], axis=0)
            part = jnp.dot(
                block[:, :half], down_a[...], preferred_element_type=jnp.float32
            ) + jnp.dot(block[:, half:], down_b[...], preferred_element_type=jnp.float32)
            acc[...] = part if i == 0 else acc[...] + part

    @pl.when(step == RING - 1)
    def _():
        at = 0
        for color, outer in [p for g in groups for p in g]:
            for inner in range(RING):
                place = index[RING + color * RING * RING + outer * RING + inner]
                rows = PIECE // RING
                out[pl.ds(place, 1), color * rows : (color + 1) * rows, :] = acc[
                    at : at + rows, :
                ].astype(out.dtype)[None]
                at += rows


def mlp_out(index, hidden, down_a, down_b, groups):
    width = down_a.shape[1]
    depth = down_a.shape[0] // RING
    total = sum(PIECE * len(g) for g in groups)
    flat = [h for g in hidden for h in g]
    return pl.pallas_call(
        functools.partial(mlp_out_kernel, groups=groups),
        grid_spec=pltpu.PrefetchScalarGridSpec(
            num_scalar_prefetch=1,
            grid=(RING,),
            in_specs=[pl.BlockSpec(h.shape, lambda k, ix: (0, 0)) for h in flat]
            + [pl.BlockSpec((depth, width), lambda k, ix: (ix[k], 0))] * 2,
            out_specs=pl.BlockSpec((RING * RING, total // RING // RING, width), lambda k, ix: (0, 0, 0)),
            scratch_shapes=[pltpu.VMEM((total, width), jnp.float32)],
        ),
        out_shape=jax.ShapeDtypeStruct((RING * RING, total // RING // RING, width), jnp.bfloat16),
        name="mlp_out",
    )(index, *flat, down_a, down_b)


def shards(
    hidden_in,
    query,
    incoming_key,
    incoming_value,
    private_tail_keys,
    private_tail_values,
    group_prompt_keys,
    group_prompt_values,
    group_id,
    prompt_len,
    tail_len,
    out_proj,
    norm_gain,
    gate_proj,
    up_proj,
    down_proj,
):
    gate_other = shift(gate_proj, "core", 1)
    up_other = shift(up_proj, "core", 1)
    down_other = shift(down_proj, "core", 1)
    n_req = lax.axis_size(REQ)
    n_head = lax.axis_size("head")
    row_count = query.shape[0]
    kv_local = incoming_key.shape[1] // HEAD_WIDTH
    each_key_value = QUERY_HEADS // KEY_VALUE_HEADS
    group_count = prompt_len.shape[0]
    prompt_size = group_prompt_keys.shape[1]
    tail_size = private_tail_keys.shape[1]
    slot_cap = 2 * row_count // n_req
    slot_total = n_req * slot_cap
    scale_of_scores = HEAD_WIDTH ** (-0.5)
    col_width = query.shape[1]
    head_local = kv_local * each_key_value
    holder = group_id // group_count
    local_group = group_id - holder * group_count
    holder_hot = (holder[:, None] == jnp.arange(n_req)[None, :]).astype(jnp.int32)
    before = jnp.cumsum(holder_hot, axis=0) - holder_hot
    order_in = jnp.sum(before * holder_hot, axis=1)
    slot_of = holder * slot_cap + order_in
    placing = slot_of[:, None] == jnp.arange(slot_total)[None, :]
    sent_rows = jnp.einsum(
        "rs,rc->sc",
        placing.astype(jnp.bfloat16),
        jnp.concatenate(
            [
                query,
                jnp.broadcast_to(
                    (local_group[:, None] + 1).astype(jnp.bfloat16), (row_count, HEAD_WIDTH)
                ),
            ],
            axis=1,
        ),
        preferred_element_type=jnp.float32,
    ).astype(jnp.bfloat16)
    keys_all = group_prompt_keys.reshape(group_count * prompt_size, kv_local, HEAD_WIDTH)
    values_all = group_prompt_values.reshape(group_count * prompt_size, kv_local, HEAD_WIDTH)
    key_group = jnp.arange(group_count * prompt_size) // prompt_size
    key_live = jnp.arange(group_count * prompt_size) % prompt_size < jnp.repeat(
        prompt_len, prompt_size
    )
    recv = lax.all_to_all(
        sent_rows.reshape(n_req, slot_cap, col_width + HEAD_WIDTH),
        REQ,
        split_axis=0,
        concat_axis=0,
        tiled=True,
    ).reshape(slot_total, col_width + HEAD_WIDTH)
    recv_group = recv[:, col_width].astype(jnp.int32) - 1
    flat_query = recv[:, :col_width].reshape(slot_total, kv_local, each_key_value, HEAD_WIDTH)
    scores = (
        jnp.einsum("nkrd,pkd->nkrp", flat_query, keys_all, preferred_element_type=jnp.float32)
        * scale_of_scores
    )
    usable = (recv_group[:, None] == key_group[None, :]) & key_live[
        None, :
    ]
    masked = jnp.where(usable[:, None, None, :], scores, MASKED_SCORE)
    largest = jnp.max(masked, axis=-1)
    weights = jnp.exp(masked - largest[..., None])
    totals = jnp.sum(weights, axis=-1)
    mixture = jnp.einsum(
        "nkrp,pkd->nkrd",
        weights.astype(jnp.bfloat16),
        values_all,
        preferred_element_type=jnp.float32,
    )
    back = lax.all_to_all(
        jnp.concatenate(
            [
                mixture.reshape(slot_total, col_width),
                largest.reshape(slot_total, head_local),
                totals.reshape(slot_total, head_local),
                jnp.zeros((slot_total, HEAD_WIDTH - 2 * head_local), jnp.float32),
            ],
            axis=1,
        ).reshape(n_req, slot_cap, col_width + HEAD_WIDTH),
        REQ,
        split_axis=0,
        concat_axis=0,
        tiled=True,
    )
    shared = jnp.take(back.reshape(slot_total, col_width + HEAD_WIDTH), slot_of, axis=0)
    shared_mix = shared[:, :col_width].reshape(row_count, kv_local, each_key_value, HEAD_WIDTH)
    shared_max = shared[:, col_width : col_width + head_local].reshape(
        row_count, kv_local, each_key_value
    )
    shared_total = shared[:, col_width + head_local : col_width + 2 * head_local].reshape(
        row_count, kv_local, each_key_value
    )
    query_rows = query.reshape(row_count, kv_local, each_key_value, HEAD_WIDTH)
    request_keys = private_tail_keys.reshape(row_count, tail_size, kv_local, HEAD_WIDTH)
    request_values = private_tail_values.reshape(row_count, tail_size, kv_local, HEAD_WIDTH)
    tail_scores = (
        jnp.einsum("bkrd,btkd->bkrt", query_rows, request_keys, preferred_element_type=jnp.float32)
        * scale_of_scores
    )
    current_scores = (
        jnp.einsum(
            "ivxg,ivg->ivx",
            query_rows,
            incoming_key.reshape(row_count, kv_local, HEAD_WIDTH),
            preferred_element_type=jnp.float32,
        )
        * scale_of_scores
    )
    tail_live = (jnp.arange(tail_size)[None, :] < tail_len[:, None])[:, None, None, :]
    tail_masked = jnp.where(tail_live, tail_scores, MASKED_SCORE)
    local_max = jnp.maximum(jnp.max(tail_masked, axis=-1), current_scores)
    tail_exp = jnp.exp(tail_masked - local_max[..., None])
    fresh_exp = jnp.exp(current_scores - local_max)
    local_total = jnp.sum(tail_exp, axis=-1) + fresh_exp
    fresh_weights = lax.optimization_barrier(fresh_exp.astype(jnp.bfloat16)).astype(jnp.float32)
    fresh_vals = incoming_value.reshape(row_count, kv_local, HEAD_WIDTH).astype(jnp.float32)
    local_mix = (
        jnp.einsum(
            "bkrt,btkd->bkrd",
            tail_exp.astype(jnp.bfloat16),
            request_values,
            preferred_element_type=jnp.float32,
        )
        + fresh_weights[..., None] * fresh_vals[:, :, None, :]
    )
    highest = jnp.maximum(shared_max, local_max)
    shared_factor = jnp.exp(shared_max - highest)
    local_factor = jnp.exp(local_max - highest)
    numer = shared_mix * shared_factor[..., None] + local_mix * local_factor[..., None]
    denom = shared_total * shared_factor + local_total * local_factor
    attention = (numer / denom[..., None]).reshape(row_count, col_width).astype(jnp.bfloat16)
    projected = jnp.dot(attention, out_proj, preferred_element_type=jnp.float32)
    sub_rows = row_count // n_head
    head_index = lax.axis_index("head")
    parts = lax.all_to_all(
        projected.astype(jnp.bfloat16).reshape(n_head, sub_rows, -1),
        "head",
        split_axis=0,
        concat_axis=0,
        tiled=True,
    )
    own_in = lax.dynamic_slice_in_dim(hidden_in, head_index * sub_rows, sub_rows, 0)
    residual = (
        own_in.astype(jnp.float32) + jnp.sum(parts.astype(jnp.float32), axis=0)
    ).astype(jnp.bfloat16)
    resid_f = residual.astype(jnp.float32)
    normed = (
        resid_f
        * lax.rsqrt(jnp.mean(resid_f * resid_f, axis=-1, keepdims=True) + 1e-05)
        * norm_gain
    ).astype(jnp.bfloat16)
    block = lax.all_gather(normed, "head", axis=0, tiled=True)
    half = row_count // 2
    first_a = jnp.concatenate(ring_pieces(block[:half], "x"), axis=0)
    first_b = jnp.concatenate(ring_pieces(block[half:], "y"), axis=0)
    pieces = (ring_pieces(first_a, "y"), ring_pieces(first_b, "x"))
    groups = (((0, 0), (1, 0)), ((0, 1), (0, 3), (1, 1), (1, 3)), ((0, 2), (1, 2)))
    hidden = [
        ring_pieces(
            mlp_in([pieces[c][d] for c, d in g], (gate_proj, gate_other, up_proj, up_other)), "head"
        )
        for g in groups
    ]
    steps = jnp.arange(RING, dtype=jnp.int32)
    at_y = (lax.axis_index("y") - steps) % RING
    at_x = (lax.axis_index("x") - steps) % RING
    index = jnp.concatenate(
        [
            (head_index - steps) % RING,
            (at_y[:, None] * RING + at_x[None, :]).reshape(-1),
            (at_y[None, :] * RING + at_x[:, None]).reshape(-1),
        ]
    )
    partial = mlp_out(index, hidden, down_proj, down_other, groups)
    lowered = lax.all_to_all(
        partial.reshape(RING * RING * n_head, sub_rows, -1),
        ("y", "x", "head"),
        split_axis=0,
        concat_axis=0,
        tiled=True,
    ).reshape(RING * RING, n_head, sub_rows, -1)
    lowered = jnp.sum(lowered.astype(jnp.float32), axis=0)
    lowered = jnp.swapaxes(lowered, 0, 1).reshape(sub_rows, -1)
    return (resid_f + lowered).astype(jnp.bfloat16)


def solution(mesh):
    mesh = Mesh(mesh.devices.reshape(RING, RING, 2, mesh.devices.shape[1]), REQ + ("head",))
    return jax.shard_map(
        shards,
        mesh=mesh,
        in_specs=(
            P(REQ, None),
            P(REQ, "head"),
            P(REQ, "head"),
            P(REQ, "head"),
            P(REQ, None, "head"),
            P(REQ, None, "head"),
            P(REQ, None, "head"),
            P(REQ, None, "head"),
            P(REQ),
            P(REQ),
            P(REQ),
            P("head", None),
            P(),
            P(None, REQ + ("head",)),
            P(None, REQ + ("head",)),
            P(REQ, "head"),
        ),
        out_specs=P(REQ + ("head",), None),
        check_vma=False,
    )
```

```python
import functools

import jax
import jax.numpy as jnp
from jax import lax
from jax.experimental import pallas as pl
from jax.experimental.pallas import tpu as pltpu
from jax.sharding import Mesh, PartitionSpec as P

QUERY_HEADS = 32
KEY_VALUE_HEADS = 8
HEAD_WIDTH = 128


MASKED_SCORE = -1e30


REQ = ("y", "x", "core")
RING = 4
PIECE = 64
K_BLOCK = 512


def shift(value, axis, step):
    size = lax.axis_size(axis)
    return lax.ppermute(value, axis, [(i, (i + step) % size) for i in range(size)])


def ring_pieces(value, axis):
    return [value] + [shift(value, axis, step) for step in (1, 2, 3)]


def mlp_in_kernel(*refs, n):
    rows, (gate_a, gate_b, up_a, up_b, out, acc) = refs[:n], refs[n:]
    step = pl.program_id(0)
    block = jnp.concatenate([r[...] for r in rows], axis=0)
    width = gate_a.shape[1]
    for i, w in enumerate((gate_a, gate_b, up_a, up_b)):
        part = jnp.dot(block, w[...], preferred_element_type=jnp.float32)
        cols = pl.ds(i * width, width)

        @pl.when(step == 0)
        def _():
            acc[:, cols] = part

        @pl.when(step > 0)
        def _():
            acc[:, cols] += part

    @pl.when(step == pl.num_programs(0) - 1)
    def _():
        gate = acc[:, : 2 * width]
        out[...] = (gate / (1.0 + jnp.exp(-gate)) * acc[:, 2 * width :]).astype(out.dtype)


def mlp_in(pieces, weights):
    n = len(pieces)
    depth, width = weights[0].shape
    rows = sum(p.shape[0] for p in pieces)
    return pl.pallas_call(
        functools.partial(mlp_in_kernel, n=n),
        grid=(depth // K_BLOCK,),
        in_specs=[pl.BlockSpec((p.shape[0], K_BLOCK), lambda k: (0, k)) for p in pieces]
        + [pl.BlockSpec((K_BLOCK, width), lambda k: (k, 0))] * 4,
        out_specs=pl.BlockSpec((rows, 2 * width), lambda k: (0, 0)),
        out_shape=jax.ShapeDtypeStruct((rows, 2 * width), jnp.bfloat16),
        scratch_shapes=[pltpu.VMEM((rows, 4 * width), jnp.float32)],
        name="mlp_in",
    )(*pieces, *weights)


def mlp_out_kernel(index, *refs, groups):
    hidden, (down_a, down_b, out, acc) = refs[: RING * len(groups)], refs[RING * len(groups) :]
    step = pl.program_id(0)
    half = down_a.shape[0]
    for i in range(RING):

        @pl.when(step == i)
        def _():
            block = jnp.concatenate([hidden[g * RING + i][...] for g in range(len(groups))], axis=0)
            part = jnp.dot(
                block[:, :half], down_a[...], preferred_element_type=jnp.float32
            ) + jnp.dot(block[:, half:], down_b[...], preferred_element_type=jnp.float32)
            acc[...] = part if i == 0 else acc[...] + part

    @pl.when(step == RING - 1)
    def _():
        at = 0
        for color, outer in [p for g in groups for p in g]:
            for inner in range(RING):
                place = index[RING + color * RING * RING + outer * RING + inner]
                rows = PIECE // RING
                out[pl.ds(place, 1), color * rows : (color + 1) * rows, :] = acc[
                    at : at + rows, :
                ].astype(out.dtype)[None]
                at += rows


def mlp_out(index, hidden, down_a, down_b, groups):
    width = down_a.shape[1]
    depth = down_a.shape[0] // RING
    total = sum(PIECE * len(g) for g in groups)
    flat = [h for g in hidden for h in g]
    return pl.pallas_call(
        functools.partial(mlp_out_kernel, groups=groups),
        grid_spec=pltpu.PrefetchScalarGridSpec(
            num_scalar_prefetch=1,
            grid=(RING,),
            in_specs=[pl.BlockSpec(h.shape, lambda k, ix: (0, 0)) for h in flat]
            + [pl.BlockSpec((depth, width), lambda k, ix: (ix[k], 0))] * 2,
            out_specs=pl.BlockSpec((RING * RING, total // RING // RING, width), lambda k, ix: (0, 0, 0)),
            scratch_shapes=[pltpu.VMEM((total, width), jnp.float32)],
        ),
        out_shape=jax.ShapeDtypeStruct((RING * RING, total // RING // RING, width), jnp.bfloat16),
        name="mlp_out",
    )(index, *flat, down_a, down_b)


def shards(
    hidden_in,
    query,
    incoming_key,
    incoming_value,
    private_tail_keys,
    private_tail_values,
    group_prompt_keys,
    group_prompt_values,
    group_id,
    prompt_len,
    tail_len,
    out_proj,
    norm_gain,
    gate_proj,
    up_proj,
    down_proj,
):
    gate_other = shift(gate_proj, "core", 1)
    up_other = shift(up_proj, "core", 1)
    down_other = shift(down_proj, "core", 1)
    n_req = lax.axis_size(REQ)
    n_head = lax.axis_size("head")
    row_count = query.shape[0]
    kv_local = incoming_key.shape[1] // HEAD_WIDTH
    each_key_value = QUERY_HEADS // KEY_VALUE_HEADS
    group_count = prompt_len.shape[0]
    prompt_size = group_prompt_keys.shape[1]
    tail_size = private_tail_keys.shape[1]
    slot_cap = 2 * row_count // n_req
    slot_total = n_req * slot_cap
    scale_of_scores = HEAD_WIDTH ** (-0.5)
    col_width = query.shape[1]
    head_local = kv_local * each_key_value
    holder = group_id // group_count
    local_group = group_id - holder * group_count
    holder_hot = (holder[:, None] == jnp.arange(n_req)[None, :]).astype(jnp.int32)
    before = jnp.cumsum(holder_hot, axis=0) - holder_hot
    order_in = jnp.sum(before * holder_hot, axis=1)
    slot_of = holder * slot_cap + order_in
    placing = slot_of[:, None] == jnp.arange(slot_total)[None, :]
    sent_rows = jnp.einsum(
        "rs,rc->sc",
        placing.astype(jnp.bfloat16),
        jnp.concatenate(
            [
                query,
                jnp.broadcast_to(
                    (local_group[:, None] + 1).astype(jnp.bfloat16), (row_count, HEAD_WIDTH)
                ),
            ],
            axis=1,
        ),
        preferred_element_type=jnp.float32,
    ).astype(jnp.bfloat16)
    keys_all = group_prompt_keys.reshape(group_count * prompt_size, kv_local, HEAD_WIDTH)
    values_all = group_prompt_values.reshape(group_count * prompt_size, kv_local, HEAD_WIDTH)
    key_group = jnp.arange(group_count * prompt_size) // prompt_size
    key_live = jnp.arange(group_count * prompt_size) % prompt_size < jnp.repeat(
        prompt_len, prompt_size
    )
    recv = lax.all_to_all(
        sent_rows.reshape(n_req, slot_cap, col_width + HEAD_WIDTH),
        REQ,
        split_axis=0,
        concat_axis=0,
        tiled=True,
    ).reshape(slot_total, col_width + HEAD_WIDTH)
    recv_group = recv[:, col_width].astype(jnp.int32) - 1
    flat_query = recv[:, :col_width].reshape(slot_total, kv_local, each_key_value, HEAD_WIDTH)
    scores = (
        jnp.einsum("nkrd,pkd->nkrp", flat_query, keys_all, preferred_element_type=jnp.float32)
        * scale_of_scores
    )
    usable = (recv_group[:, None] == key_group[None, :]) & key_live[
        None, :
    ]
    masked = jnp.where(usable[:, None, None, :], scores, MASKED_SCORE)
    largest = jnp.max(masked, axis=-1)
    weights = jnp.exp(masked - largest[..., None])
    totals = jnp.sum(weights, axis=-1)
    mixture = jnp.einsum(
        "nkrp,pkd->nkrd",
        weights.astype(jnp.bfloat16),
        values_all,
        preferred_element_type=jnp.float32,
    )
    back = lax.all_to_all(
        jnp.concatenate(
            [
                mixture.reshape(slot_total, col_width),
                largest.reshape(slot_total, head_local),
                totals.reshape(slot_total, head_local),
                jnp.zeros((slot_total, HEAD_WIDTH - 2 * head_local), jnp.float32),
            ],
            axis=1,
        ).reshape(n_req, slot_cap, col_width + HEAD_WIDTH),
        REQ,
        split_axis=0,
        concat_axis=0,
        tiled=True,
    )
    shared = jnp.take(back.reshape(slot_total, col_width + HEAD_WIDTH), slot_of, axis=0)
    shared_mix = shared[:, :col_width].reshape(row_count, kv_local, each_key_value, HEAD_WIDTH)
    shared_max = shared[:, col_width : col_width + head_local].reshape(
        row_count, kv_local, each_key_value
    )
    shared_total = shared[:, col_width + head_local : col_width + 2 * head_local].reshape(
        row_count, kv_local, each_key_value
    )
    query_rows = query.reshape(row_count, kv_local, each_key_value, HEAD_WIDTH)
    request_keys = private_tail_keys.reshape(row_count, tail_size, kv_local, HEAD_WIDTH)
    request_values = private_tail_values.reshape(row_count, tail_size, kv_local, HEAD_WIDTH)
    tail_scores = (
        jnp.einsum("bkrd,btkd->bkrt", query_rows, request_keys, preferred_element_type=jnp.float32)
        * scale_of_scores
    )
    current_scores = (
        jnp.einsum(
            "ivxg,ivg->ivx",
            query_rows,
            incoming_key.reshape(row_count, kv_local, HEAD_WIDTH),
            preferred_element_type=jnp.float32,
        )
        * scale_of_scores
    )
    tail_live = (jnp.arange(tail_size)[None, :] < tail_len[:, None])[:, None, None, :]
    tail_masked = jnp.where(tail_live, tail_scores, MASKED_SCORE)
    local_max = jnp.maximum(jnp.max(tail_masked, axis=-1), current_scores)
    tail_exp = jnp.exp(tail_masked - local_max[..., None])
    fresh_exp = jnp.exp(current_scores - local_max)
    local_total = jnp.sum(tail_exp, axis=-1) + fresh_exp
    fresh_weights = lax.optimization_barrier(fresh_exp.astype(jnp.bfloat16)).astype(jnp.float32)
    fresh_vals = incoming_value.reshape(row_count, kv_local, HEAD_WIDTH).astype(jnp.float32)
    local_mix = (
        jnp.einsum(
            "bkrt,btkd->bkrd",
            tail_exp.astype(jnp.bfloat16),
            request_values,
            preferred_element_type=jnp.float32,
        )
        + fresh_weights[..., None] * fresh_vals[:, :, None, :]
    )
    highest = jnp.maximum(shared_max, local_max)
    shared_factor = jnp.exp(shared_max - highest)
    local_factor = jnp.exp(local_max - highest)
    numer = shared_mix * shared_factor[..., None] + local_mix * local_factor[..., None]
    denom = shared_total * shared_factor + local_total * local_factor
    attention = (numer / denom[..., None]).reshape(row_count, col_width).astype(jnp.bfloat16)
    projected = jnp.dot(attention, out_proj, preferred_element_type=jnp.float32)
    sub_rows = row_count // n_head
    head_index = lax.axis_index("head")
    parts = lax.all_to_all(
        projected.astype(jnp.bfloat16).reshape(n_head, sub_rows, -1),
        "head",
        split_axis=0,
        concat_axis=0,
        tiled=True,
    )
    own_in = lax.dynamic_slice_in_dim(hidden_in, head_index * sub_rows, sub_rows, 0)
    residual = (
        own_in.astype(jnp.float32) + jnp.sum(parts.astype(jnp.float32), axis=0)
    ).astype(jnp.bfloat16)
    resid_f = residual.astype(jnp.float32)
    normed = (
        resid_f
        * lax.rsqrt(jnp.mean(resid_f * resid_f, axis=-1, keepdims=True) + 1e-05)
        * norm_gain
    ).astype(jnp.bfloat16)
    from_head = ring_pieces(normed, "head")
    block = jnp.concatenate(
        [lax.select_n((head_index - i) % n_head, *from_head) for i in range(RING)], axis=0
    )
    half = row_count // 2
    first_a = jnp.concatenate(ring_pieces(block[:half], "x"), axis=0)
    first_b = jnp.concatenate(ring_pieces(block[half:], "y"), axis=0)
    pieces = (ring_pieces(first_a, "y"), ring_pieces(first_b, "x"))
    groups = (((0, 0), (1, 0)), ((0, 1), (0, 3), (1, 1), (1, 3)), ((0, 2), (1, 2)))
    hidden = [
        ring_pieces(
            mlp_in([pieces[c][d] for c, d in g], (gate_proj, gate_other, up_proj, up_other)), "head"
        )
        for g in groups
    ]
    steps = jnp.arange(RING, dtype=jnp.int32)
    at_y = (lax.axis_index("y") - steps) % RING
    at_x = (lax.axis_index("x") - steps) % RING
    index = jnp.concatenate(
        [
            (head_index - steps) % RING,
            (at_y[:, None] * RING + at_x[None, :]).reshape(-1),
            (at_y[None, :] * RING + at_x[:, None]).reshape(-1),
        ]
    )
    partial = mlp_out(index, hidden, down_proj, down_other, groups)
    lowered = lax.all_to_all(
        partial.reshape(RING * RING * n_head, sub_rows, -1),
        ("y", "x", "head"),
        split_axis=0,
        concat_axis=0,
        tiled=True,
    ).reshape(RING * RING, n_head, sub_rows, -1)
    lowered = jnp.sum(lowered.astype(jnp.float32), axis=0)
    lowered = jnp.swapaxes(lowered, 0, 1).reshape(sub_rows, -1)
    return (resid_f + lowered).astype(jnp.bfloat16)


def solution(mesh):
    mesh = Mesh(mesh.devices.reshape(RING, RING, 2, mesh.devices.shape[1]), REQ + ("head",))
    return jax.shard_map(
        shards,
        mesh=mesh,
        in_specs=(
            P(REQ, None),
            P(REQ, "head"),
            P(REQ, "head"),
            P(REQ, "head"),
            P(REQ, None, "head"),
            P(REQ, None, "head"),
            P(REQ, None, "head"),
            P(REQ, None, "head"),
            P(REQ),
            P(REQ),
            P(REQ),
            P("head", None),
            P(),
            P(None, REQ + ("head",)),
            P(None, REQ + ("head",)),
            P(REQ, "head"),
        ),
        out_specs=P(REQ + ("head",), None),
        check_vma=False,
    )
```
